768 devices in a mesh: inner: 8 (over y), outer: 24 (over x_hi, z), head: 4 (over x_lo, core).
Axes of the slice: x: 4 (x_hi: 2, x_lo: 2; x = x_hi * 2 + x_lo), y: 8, z: 12, core: 2. Of those that a mesh axis runs over, the one named last changes fastest.
Arguments:
- queries: bfloat16 [49152, 64, 128], P(('inner', 'outer', 'head')), may hold values from -6 to 6
- key_vector_rows: bfloat16 [49152, 8, 128], P(('inner', 'outer'), 'head'), may hold values from -6 to 6
- value_vector_rows: bfloat16 [49152, 8, 128], P(('inner', 'outer'), 'head'), may hold values from -6 to 6
- grad_out: bfloat16 [49152, 64, 128], P(('inner', 'outer', 'head')), may hold values from -24 to 24
Outputs:
- query_grads: bfloat16 [49152, 64, 128], P(('inner', 'outer', 'head'))
- key_gradient_rows: bfloat16 [49152, 8, 128], P(('inner', 'outer'), 'head')
- value_gradient_rows: bfloat16 [49152, 8, 128], P(('inner', 'outer'), 'head')
The draws below stay inside these ranges and needn't reach their ends.
All inputs are finite; a program needn't handle non-finite values.
Results may differ from the reference program's by a relative error of at most 0.012.
Values may be sent and summed in bfloat16 or wider, within the bound.
A program may use at most 64 MiB of HBM per device.

```python
import jax
import jax.numpy as jnp
from jax import lax

QUERY_HEADS = 64
KEY_VALUE_HEADS = 8
HEAD_WIDTH = 128
BLOCK_TOKENS = 256
SEQUENCE_TOKENS = 49152


def paired_draw(key):
    queries = jax.random.truncated_normal(jax.random.fold_in(key, 21), -6.0, 6.0, (SEQUENCE_TOKENS, QUERY_HEADS, HEAD_WIDTH), jnp.float32)
    key_vector_rows = jax.random.truncated_normal(jax.random.fold_in(key, 22), -6.0, 6.0, (SEQUENCE_TOKENS, KEY_VALUE_HEADS, HEAD_WIDTH), jnp.float32)
    return (queries, key_vector_rows)


def draw_queries(key, part):
    return paired_draw(key)[0].astype(jnp.bfloat16)


def draw_key_vector_rows(key, part):
    return paired_draw(key)[1].astype(jnp.bfloat16)


def levels(rng, dims, shards, least, largest):
    def one(position, blocks):
        heights = jax.random.uniform(jax.random.fold_in(jax.random.fold_in(rng, 6), position), (blocks,), jnp.float32, least / len(shards), largest / len(shards))
        return jnp.repeat(jnp.exp(heights), dims[position] // blocks).reshape((-1,) + (1,) * (len(dims) - position - 1))

    loudness = one(*shards[0])
    for cut in shards[1:]:
        loudness = loudness * one(*cut)
    return loudness


def noise(rng, dims, deviation, most, cuts=(), kind=jnp.bfloat16):
    entries = deviation * jax.random.normal(rng, dims, jnp.float32)
    if cuts:
        entries = entries * levels(rng, dims, cuts, -0.22, 0.18)
    return jnp.clip(entries, -most, most).astype(kind)


def setup_inputs(seed: int = 0) -> dict:
    seeds = jax.random.split(jax.random.key(seed), 5)
    queries = draw_queries(jax.random.fold_in(seeds[4], 71), 0)
    key_vector_rows = draw_key_vector_rows(jax.random.fold_in(seeds[4], 71), 0)
    value_vector_rows = noise(seeds[2], (SEQUENCE_TOKENS, KEY_VALUE_HEADS, HEAD_WIDTH), 1.0, 6.0, ((0, 192), (1, 4)))
    grad_out = noise(seeds[3], (SEQUENCE_TOKENS, QUERY_HEADS, HEAD_WIDTH), 4.0, 24.0, ((0, 768),))
    return {"queries": queries, "key_vector_rows": key_vector_rows, "value_vector_rows": value_vector_rows, "grad_out": grad_out}


def head_grads(query_part, grad_part, key_part, value_part, allowed):
    softmax_scale = query_part.shape[-1] ** -0.5
    query_wide = query_part.astype(jnp.float32)
    grad_wide = grad_part.astype(jnp.float32)
    key_wide = key_part.astype(jnp.float32)
    value_wide = value_part.astype(jnp.float32)
    scores = jnp.einsum('rgd,kd->grk', query_wide, key_wide) * softmax_scale
    scores = jnp.where(allowed[None], scores, -jnp.inf)
    highest = jnp.max(scores, axis=-1, keepdims=True)
    probs = jnp.exp(scores - highest)
    probs = probs / jnp.sum(probs, axis=-1, keepdims=True)
    probs_low = lax.optimization_barrier(probs.astype(jnp.bfloat16)).astype(jnp.float32)
    value_gradient_rows = jnp.einsum('grk,rgd->kd', probs_low, grad_wide)
    dprobs = jnp.einsum('rgd,kd->grk', grad_wide, value_wide)
    delta = jnp.sum(probs * dprobs, axis=-1, keepdims=True)
    dscores = lax.optimization_barrier((probs * (dprobs - delta)).astype(jnp.bfloat16)).astype(jnp.float32)
    query_grads = jnp.einsum('grk,kd->rgd', dscores, key_wide) * softmax_scale
    key_gradient_rows = jnp.einsum('grk,rgd->kd', dscores, query_wide) * softmax_scale
    return query_grads, key_gradient_rows, value_gradient_rows


def block_grads(query_rows, grad_rows, key_window, value_window, allowed):
    row_count, head_count, width = query_rows.shape
    group_count = key_window.shape[1]
    heads_per_group = head_count // group_count
    query_split = query_rows.reshape(row_count, group_count, heads_per_group, width).transpose(1, 0, 2, 3)
    grad_split = grad_rows.reshape(row_count, group_count, heads_per_group, width).transpose(1, 0, 2, 3)
    key_split = key_window.transpose(1, 0, 2)
    value_split = value_window.transpose(1, 0, 2)
    query_grads, key_gradient_rows, value_gradient_rows = lax.map(lambda packed: head_grads(packed[0], packed[1], packed[2], packed[3], allowed), (query_split, grad_split, key_split, value_split))
    query_grads = query_grads.transpose(1, 0, 2, 3).reshape(row_count, head_count, width)
    return query_grads, key_gradient_rows.transpose(1, 0, 2), value_gradient_rows.transpose(1, 0, 2)


def reference(queries, key_vector_rows, value_vector_rows, grad_out):
    blocks = SEQUENCE_TOKENS // BLOCK_TOKENS
    query_blocks = queries.reshape(blocks, BLOCK_TOKENS, QUERY_HEADS, HEAD_WIDTH)
    grad_blocks = grad_out.reshape(blocks, BLOCK_TOKENS, QUERY_HEADS, HEAD_WIDTH)
    padding_rows = jnp.zeros((2 * BLOCK_TOKENS, KEY_VALUE_HEADS, HEAD_WIDTH), jnp.bfloat16)
    key_padded = jnp.concatenate([padding_rows, key_vector_rows], axis=0)
    value_padded = jnp.concatenate([padding_rows, value_vector_rows], axis=0)

    def step(carry, index):
        first_k, first_v, second_k, second_v = carry
        start = (index * BLOCK_TOKENS).astype(jnp.int32)
        key_window = lax.dynamic_slice_in_dim(key_padded, start, 3 * BLOCK_TOKENS, 0)
        value_window = lax.dynamic_slice_in_dim(value_padded, start, 3 * BLOCK_TOKENS, 0)
        query_positions = index * BLOCK_TOKENS + jnp.arange(BLOCK_TOKENS, dtype=jnp.int32)
        key_positions = (index - 2) * BLOCK_TOKENS + jnp.arange(3 * BLOCK_TOKENS, dtype=jnp.int32)
        allowed = (key_positions[None, :] <= query_positions[:, None]) & (key_positions[None, :] >= 0)
        query_block = lax.dynamic_index_in_dim(query_blocks, index, 0, keepdims=False)
        grad_block = lax.dynamic_index_in_dim(grad_blocks, index, 0, keepdims=False)
        query_grads, key_gradient_rows, value_gradient_rows = block_grads(query_block, grad_block, key_window, value_window, allowed)
        key_slot_rows = key_gradient_rows.reshape(3, BLOCK_TOKENS, KEY_VALUE_HEADS, HEAD_WIDTH)
        value_slot_rows = value_gradient_rows.reshape(3, BLOCK_TOKENS, KEY_VALUE_HEADS, HEAD_WIDTH)
        finished = (first_k + key_slot_rows[0], first_v + value_slot_rows[0])
        carry_next = (second_k + key_slot_rows[1], second_v + value_slot_rows[1], key_slot_rows[2], value_slot_rows[2])
        return carry_next, (query_grads.astype(jnp.bfloat16), finished[0], finished[1])

    zero_filled = jnp.zeros((BLOCK_TOKENS, KEY_VALUE_HEADS, HEAD_WIDTH), jnp.float32)
    final_result, output_list = lax.scan(step, (zero_filled, zero_filled, zero_filled, zero_filled), jnp.arange(blocks, dtype=jnp.int32))
    query_grads = output_list[0].reshape(SEQUENCE_TOKENS, QUERY_HEADS, HEAD_WIDTH)
    key_gradient_rows = jnp.concatenate([output_list[1][2:].reshape(-1, KEY_VALUE_HEADS, HEAD_WIDTH), final_result[0], final_result[2]], axis=0)
    value_gradient_rows = jnp.concatenate([output_list[2][2:].reshape(-1, KEY_VALUE_HEADS, HEAD_WIDTH), final_result[1], final_result[3]], axis=0)
    return query_grads, key_gradient_rows.astype(jnp.bfloat16), value_gradient_rows.astype(jnp.bfloat16)
```

```python
import functools

import jax
import jax.numpy as jnp
from jax import lax
from jax.experimental import pallas as pl
from jax.experimental.pallas import tpu as pltpu
from jax.sharding import PartitionSpec as P

MESH = pl.DeviceIdType.MESH
SCALE = 128**-0.5
LOG2E = 1.4426950408889634
MASKED = -1e30
ROWS = 512


def dot(a, b, a_dim, b_dim):
    return lax.dot_general(
        a, b, (((a_dim,), (b_dim,)), ((), ())), preferred_element_type=jnp.float32
    )


def unit_grads(kv, q_ref, g_ref, dq_ref, acc, s_ref, d_ref, first_token, far_off, near_off):
    offs = (far_off, near_off, None)
    tokens, heads, width = q_ref.shape
    per = ROWS // heads
    for i in range(tokens // per):
        part = pl.ds(i * per, per)
        q = q_ref[part].reshape(ROWS, width)
        g = g_ref[part].reshape(ROWS, width)
        highest = None
        for s in range(3):
            x = dot(kv[s][0][...], q, 1, 1)
            if s == 2:
                key = lax.broadcasted_iota(jnp.int32, x.shape, 0) * heads
                row = lax.broadcasted_iota(jnp.int32, x.shape, 1)
                x = jnp.where(key - row <= heads * first_token + i * ROWS, x, MASKED)
            s_ref[s] = x
            top = jnp.max(x, axis=0, keepdims=True)
            if offs[s] is not None:
                top = top - offs[s]
            highest = top if highest is None else jnp.maximum(highest, top)
        total = jnp.zeros((1, ROWS), jnp.float32)
        delta = jnp.zeros((1, ROWS), jnp.float32)
        for s in range(3):
            base = highest if offs[s] is None else highest + offs[s]
            e = jnp.exp2((s_ref[s] - base) * (SCALE * LOG2E))
            s_ref[s] = e
            total = total + jnp.sum(e, axis=0, keepdims=True)
            dp = dot(kv[s][1][...], g, 1, 1)
            d_ref[s] = dp
            delta = delta + jnp.sum(e * dp, axis=0, keepdims=True)
        inverse = 1.0 / total
        delta = delta * inverse
        dq = None
        for s in range(3):
            probs = s_ref[s] * inverse
            low = probs.astype(jnp.bfloat16)
            ds = (probs * (d_ref[s] - delta)).astype(jnp.bfloat16)
            dv = dot(low, g, 1, 0)
            dk = dot(ds, q, 1, 0) * SCALE
            if i == 0:
                acc[s][1][...] = dv
                acc[s][0][...] = dk
            else:
                acc[s][1][...] += dv
                acc[s][0][...] += dk
            term = dot(ds, kv[s][0][...], 0, 0)
            dq = term if dq is None else dq + term
        dq_ref[part] = (dq * SCALE).astype(jnp.bfloat16).reshape(per, heads, width)


def kernel(
    sizes,
    q_in, g_in, k_in, v_in,
    dq_out, dk_out, dv_out,
    kvb, qb, gb, dqb, acc, s_ref, d_ref, xs, xr, zs, zr,
    own_sem, kvown_sem, qg_send, qg_recv,
    z1_send, z1_recv, z0_send, z0_recv, x2_send, x2_recv, x_send, x_recv,
    dqown_sem, dq_send, dq_recv, xg_send, xg_recv, zg_send, zg_recv,
):
    n_inner, n_outer = sizes
    n_z = n_outer // 2
    blocks = n_inner * n_outer
    inner, outer, head = lax.axis_index("inner"), lax.axis_index("outer"), lax.axis_index("head")
    p, c = head // 2, head % 2
    z = outer % n_z
    block = inner * n_outer + outer
    turn_next = 1 - jnp.minimum(n_z - 1 - z, 1)
    turn_here = 1 - jnp.minimum(z, 1)
    turn_prev = 1 - jnp.minimum((z - 1) * (z - 1), 1)
    half = ((p + turn_here + turn_prev) % 2, (p + turn_here) % 2, p)

    def place(b, pp):
        return (b // n_outer, b % n_outer, pp * 2 + c)

    nxt = place((block + 1) % blocks, (p + turn_next) % 2)
    prv = place((block + blocks - 1) % blocks, (p + turn_here) % 2)
    beside = (inner, outer, (1 - p) * 2 + c)
    twin = (inner, outer, p * 2 + 1 - c)

    a = half[0]
    order = ((a, 0), (1 - a, 0), (1 - a, 1), (a, 1))

    def kv_head(u):
        h, j = order[u]
        return 4 * h + 2 * c + j

    def remote(src, dst, send, recv, device):
        return pltpu.make_async_remote_copy(
            src_ref=src, dst_ref=dst, send_sem=send, recv_sem=recv,
            device_id=device, device_id_type=MESH,
        )

    def own_copies(u):
        h, j = order[u]
        to = pl.ds(c * 64, 64)
        return [
            pltpu.make_async_copy(q_in.at[:, kv_head(u)], qb.at[h, j, to], own_sem.at[u, 0]),
            pltpu.make_async_copy(g_in.at[:, kv_head(u)], gb.at[h, j, to], own_sem.at[u, 1]),
        ]

    def kvown_copies(j):
        return [
            pltpu.make_async_copy(x.at[j], kvb.at[2, p, j, t], kvown_sem.at[j, t])
            for t, x in enumerate((k_in, v_in))
        ]

    def qg_copies(u):
        h, j = order[u]
        there = 4 * h + 2 * (1 - c) + j
        to = pl.ds(c * 64, 64)
        return [
            remote(q_in.at[:, there], qb.at[h, j, to], qg_send.at[u, 0], qg_recv.at[u, 0], twin),
            remote(g_in.at[:, there], gb.at[h, j, to], qg_send.at[u, 1], qg_recv.at[u, 1], twin),
        ]

    def z1_copies(j):
        return [
            remote(x.at[j], kvb.at[1, p, j, t], z1_send.at[j, t], z1_recv.at[j, t], nxt)
            for t, x in enumerate((k_in, v_in))
        ]

    def x2_copies(j):
        return [
            remote(x.at[j], kvb.at[2, p, j, t], x2_send.at[j, t], x2_recv.at[j, t], beside)
            for t, x in enumerate((k_in, v_in))
        ]

    def z0_copy(j):
        piece = kvb.at[1, half[1], j]
        return remote(piece, kvb.at[0, half[1], j], z0_send.at[j], z0_recv.at[j], nxt)

    def x_copy(s, j):
        piece = kvb.at[s, half[s], j]
        return remote(piece, piece, x_send.at[s, j], x_recv.at[s, j], beside)

    def xg_copy(s, j):
        return remote(xs.at[s, j], xr.at[s, j], xg_send.at[s, j], xg_recv.at[s, j], beside)

    def zg_copy(s, j):
        return remote(zs.at[s, j], zr.at[s, j], zg_send.at[s, j], zg_recv.at[s, j], prv)

    def dq_copies(u):
        h, j = order[u]
        at = kv_head(u)
        own = pltpu.make_async_copy(
            dqb.at[h, j, pl.ds(c * 64, 64)], dq_out.at[:, at], dqown_sem.at[u]
        )
        away = remote(
            dqb.at[h, j, pl.ds((1 - c) * 64, 64)], dq_out.at[:, at],
            dq_send.at[u], dq_recv.at[u], twin,
        )
        return own, away

    def start(copies):
        for copy in copies:
            copy.start()

    for u in range(4):
        start(own_copies(u))
    for j in range(2):
        start(kvown_copies(j))

    barrier = pltpu.get_barrier_semaphore()
    for peer in (twin, beside, nxt, prv):
        pl.semaphore_signal(barrier, inc=1, device_id=peer, device_id_type=MESH)
    pl.semaphore_wait(barrier, 4)

    start(z1_copies(0))
    start(x2_copies(0))
    start(qg_copies(0))
    start(qg_copies(1))

    def wait_x2(j):
        for copy in x2_copies(j):
            copy.wait_recv()

    for j in range(2):
        for copy in z1_copies(j):
            copy.wait_recv()
        z0_copy(j).start()
        x_copy(1, j).start()
        if j == 0:
            start(z1_copies(1))
            start(x2_copies(1))
            start(qg_copies(2))
            start(qg_copies(3))
    z0_copy(0).wait_recv()
    x_copy(0, 0).start()
    for j in range(2):
        for copy in kvown_copies(j):
            copy.wait()

    first_token = 128 * p
    far_off = (1 - jnp.minimum(block // 2, 1)).astype(jnp.float32) * (-MASKED)
    near_off = (1 - jnp.minimum(block, 1)).astype(jnp.float32) * (-MASKED)

    def export(s, j):
        h = 1 - half[s]
        for t in range(2):
            xs[s, j, t] = acc[s, h, j, t].astype(jnp.bfloat16)
        xg_copy(s, j).start()

    def compute(u):
        h, j = order[u]
        for copy in own_copies(u):
            copy.wait()
        for copy in qg_copies(u):
            copy.wait_recv()
        if u in (0, 3):
            @pl.when(half[1] != a)
            def _():
                x_copy(1, j).wait_recv()

            @pl.when(p != a)
            def _():
                wait_x2(j)
        else:
            x_copy(0, j).wait_recv()

            @pl.when(half[1] == a)
            def _():
                x_copy(1, j).wait_recv()

            @pl.when(p == a)
            def _():
                wait_x2(j)
        unit_grads(
            [(kvb.at[s, h, j, 0], kvb.at[s, h, j, 1]) for s in range(3)],
            qb.at[h, j], gb.at[h, j], dqb.at[h, j],
            [(acc.at[s, h, j, 0], acc.at[s, h, j, 1]) for s in range(3)],
            s_ref, d_ref, first_token, far_off, near_off,
        )
        start(dq_copies(u))

    def pass_on(s, j):
        xg_copy(s, j).wait_recv()
        if s == 1:
            zg_copy(0, j).wait_recv()
        for t in range(2):
            value = acc[s, half[s], j, t] + xr[s, j, t].astype(jnp.float32)
            if s == 1:
                value = value + zr[0, j, t].astype(jnp.float32)
            zs[s, j, t] = value.astype(jnp.bfloat16)
        zg_copy(s, j).start()

    def finish(j):
        xg_copy(2, j).wait_recv()
        zg_copy(1, j).wait_recv()
        for t, out in enumerate((dk_out, dv_out)):
            value = acc[2, p, j, t] + xr[2, j, t].astype(jnp.float32)
            out[j] = (value + zr[1, j, t].astype(jnp.float32)).astype(jnp.bfloat16)

    compute(0)
    z0_copy(1).wait_recv()
    x_copy(0, 1).start()
    compute(1)
    for s in range(3):
        export(s, 0)
    compute(2)
    export(0, 1)
    for s in (1, 2):
        pl.when(half[s] == a)(functools.partial(export, s, 1))
    pass_on(0, 0)
    compute(3)
    for s in (1, 2):
        pl.when(half[s] != a)(functools.partial(export, s, 1))
    pass_on(1, 0)
    pass_on(0, 1)
    finish(0)
    pass_on(1, 1)
    finish(1)

    for u in range(4):
        own, away = dq_copies(u)
        own.wait()
        away.wait_recv()
        away.wait_send()
        for copy in qg_copies(u):
            copy.wait_send()
    for j in range(2):
        for copy in z1_copies(j) + x2_copies(j):
            copy.wait_send()
        z0_copy(j).wait_send()
        for s in range(2):
            x_copy(s, j).wait_send()
            zg_copy(s, j).wait_send()
        for s in range(3):
            xg_copy(s, j).wait_send()


def shards(sizes, queries, key_rows, value_rows, grad_out):
    tokens, heads, width = queries.shape
    keys, groups, _ = key_rows.shape
    split = (tokens, 8, heads // 8, width)
    bf16, f32 = jnp.bfloat16, jnp.float32
    any_space = pl.BlockSpec(memory_space=pl.ANY)
    vmem = pl.BlockSpec(memory_space=pltpu.VMEM)
    dma = pltpu.SemaphoreType.DMA
    unit = (2, 2, 2 * tokens, heads // 8, width)
    dq, dk, dv = pl.pallas_call(
        functools.partial(kernel, sizes),
        out_shape=(
            jax.ShapeDtypeStruct(split, bf16),
            jax.ShapeDtypeStruct((groups, keys, width), bf16),
            jax.ShapeDtypeStruct((groups, keys, width), bf16),
        ),
        in_specs=[any_space] * 4,
        out_specs=(any_space, vmem, vmem),
        scratch_shapes=[
            pltpu.VMEM((3, 2, 2, 2, keys, width), bf16),
            pltpu.VMEM(unit, bf16),
            pltpu.VMEM(unit, bf16),
            pltpu.VMEM(unit, bf16),
            pltpu.VMEM((3, 2, 2, 2, keys, width), f32),
            pltpu.VMEM((3, keys, ROWS), f32),
            pltpu.VMEM((3, keys, ROWS), f32),
            pltpu.VMEM((3, 2, 2, keys, width), bf16),
            pltpu.VMEM((3, 2, 2, keys, width), bf16),
            pltpu.VMEM((2, 2, 2, keys, width), bf16),
            pltpu.VMEM((2, 2, 2, keys, width), bf16),
            dma((4, 2)), dma((2, 2)), dma((4, 2)), dma((4, 2)),
            dma((2, 2)), dma((2, 2)), dma((2,)), dma((2,)),
            dma((2, 2)), dma((2, 2)), dma((2, 2)), dma((2, 2)),
            dma((4,)), dma((4,)), dma((4,)),
            dma((3, 2)), dma((3, 2)), dma((2, 2)), dma((2, 2)),
        ],
        compiler_params=pltpu.CompilerParams(collective_id=0, has_side_effects=True),
        name="window_grads",
    )(
        queries.reshape(split), grad_out.reshape(split),
        key_rows.transpose(1, 0, 2), value_rows.transpose(1, 0, 2),
    )
    return dq.reshape(queries.shape), dk.transpose(1, 0, 2), dv.transpose(1, 0, 2)


def solution(mesh):
    rows = P(("inner", "outer", "head"), None, None)
    groups = P(("inner", "outer"), "head", None)
    return jax.shard_map(
        functools.partial(shards, (mesh.shape["inner"], mesh.shape["outer"])),
        mesh=mesh,
        in_specs=(rows, groups, groups, rows),
        out_specs=(rows, groups, groups),
        check_vma=False,
    )
```

```python
import functools

import jax
import jax.numpy as jnp
from jax import lax
from jax.experimental import pallas as pl
from jax.experimental.pallas import tpu as pltpu
from jax.sharding import PartitionSpec as P

MESH = pl.DeviceIdType.MESH
SCALE = 128**-0.5
LOG2E = 1.4426950408889634
MASKED = -1e30
ROWS = 512


def dot(a, b, a_dim, b_dim):
    return lax.dot_general(
        a, b, (((a_dim,), (b_dim,)), ((), ())), preferred_element_type=jnp.float32
    )


def unit_grads(kv, q_ref, g_ref, dq_ref, acc, s_ref, d_ref, first_token, far_off, near_off, between):
    offs = (far_off, near_off, None)
    tokens, heads, width = q_ref.shape
    per = ROWS // heads
    for i in range(tokens // per):
        if i:
            between()
        part = pl.ds(i * per, per)
        q = q_ref[part].reshape(ROWS, width)
        g = g_ref[part].reshape(ROWS, width)
        highest = None
        for s in range(3):
            x = dot(kv[s][0][...], q, 1, 1)
            if s == 2:
                key = lax.broadcasted_iota(jnp.int32, x.shape, 0) * heads
                row = lax.broadcasted_iota(jnp.int32, x.shape, 1)
                x = jnp.where(key - row <= heads * first_token + i * ROWS, x, MASKED)
            s_ref[s] = x
            top = jnp.max(x, axis=0, keepdims=True)
            if offs[s] is not None:
                top = top - offs[s]
            highest = top if highest is None else jnp.maximum(highest, top)
        total = jnp.zeros((1, ROWS), jnp.float32)
        delta = jnp.zeros((1, ROWS), jnp.float32)
        for s in range(3):
            base = highest if offs[s] is None else highest + offs[s]
            e = jnp.exp2((s_ref[s] - base) * (SCALE * LOG2E))
            s_ref[s] = e
            total = total + jnp.sum(e, axis=0, keepdims=True)
            dp = dot(kv[s][1][...], g, 1, 1)
            d_ref[s] = dp
            delta = delta + jnp.sum(e * dp, axis=0, keepdims=True)
        inverse = 1.0 / total
        delta = delta * inverse
        dq = None
        for s in range(3):
            probs = s_ref[s] * inverse
            low = probs.astype(jnp.bfloat16)
            ds = (probs * (d_ref[s] - delta)).astype(jnp.bfloat16)
            dv = dot(low, g, 1, 0)
            dk = dot(ds, q, 1, 0) * SCALE
            if i == 0:
                acc[s][1][...] = dv
                acc[s][0][...] = dk
            else:
                acc[s][1][...] += dv
                acc[s][0][...] += dk
            term = dot(ds, kv[s][0][...], 0, 0)
            dq = term if dq is None else dq + term
        dq_ref[part] = (dq * SCALE).astype(jnp.bfloat16).reshape(per, heads, width)


def kernel(
    sizes,
    q_in, g_in, k_in, v_in,
    dq_out, dk_out, dv_out,
    kvb, qb, gb, dqb, acc, s_ref, d_ref, raw, wide,
    far_s, far_r, near_s, near_r, xs, xr,
    raw_sem, own_sem, qg_send, qg_recv,
    near_kv_send, near_kv_recv, far_kv_send, far_kv_recv, x_kv_send, x_kv_recv,
    dqown_sem, dq_send, dq_recv,
    far_send, far_recv, near_send, near_recv, x_send, x_recv,
):
    n_inner, n_outer = sizes
    n_z = n_outer // 2
    blocks = n_inner * n_outer
    inner, outer, head = lax.axis_index("inner"), lax.axis_index("outer"), lax.axis_index("head")
    p, c = head // 2, head % 2
    z = outer % n_z
    block = inner * n_outer + outer
    turn_next = 1 - jnp.minimum(n_z - 1 - z, 1)
    turn_here = 1 - jnp.minimum(z, 1)
    turn_prev = 1 - jnp.minimum((z - 1) * (z - 1), 1)
    a = (p + turn_here + turn_prev) % 2
    h1 = (p + turn_here) % 2

    def place(b, pp):
        return (b // n_outer, b % n_outer, pp * 2 + c)

    nxt = place((block + 1) % blocks, (p + turn_next) % 2)
    prv = place((block + blocks - 1) % blocks, (p + turn_here) % 2)
    beside = (inner, outer, (1 - p) * 2 + c)
    twin = (inner, outer, p * 2 + 1 - c)
    order = ((a, 0), (1 - a, 0), (a, 1), (1 - a, 1))

    def kv_head(u):
        h, j = order[u]
        return 4 * h + 2 * c + j

    def remote(src, dst, send, recv, device):
        return pltpu.make_async_remote_copy(
            src_ref=src, dst_ref=dst, send_sem=send, recv_sem=recv,
            device_id=device, device_id_type=MESH,
        )

    def own_copies(u):
        h, j = order[u]
        to = pl.ds(c * 64, 64)
        return [
            pltpu.make_async_copy(q_in.at[:, kv_head(u)], qb.at[h, j, to], own_sem.at[u, 0]),
            pltpu.make_async_copy(g_in.at[:, kv_head(u)], gb.at[h, j, to], own_sem.at[u, 1]),
        ]

    def qg_copies(u):
        h, j = order[u]
        there = 4 * h + 2 * (1 - c) + j
        to = pl.ds(c * 64, 64)
        return [
            remote(q_in.at[:, there], qb.at[h, j, to], qg_send.at[u, 0], qg_recv.at[u, 0], twin),
            remote(g_in.at[:, there], gb.at[h, j, to], qg_send.at[u, 1], qg_recv.at[u, 1], twin),
        ]

    def near_kv(j, t):
        return remote(
            kvb.at[2, p, j, t], kvb.at[1, p, j, t],
            near_kv_send.at[j, t], near_kv_recv.at[j, t], nxt,
        )

    def far_kv(h, j, t):
        return remote(
            kvb.at[1, h, j, t], kvb.at[0, h, j, t],
            far_kv_send.at[h, j, t], far_kv_recv.at[h, j, t], nxt,
        )

    def x_kv(s, j, t):
        piece = kvb.at[s, p if s == 2 else h1, j, t]
        return remote(piece, piece, x_kv_send.at[s - 1, j, t], x_kv_recv.at[s - 1, j, t], beside)

    def far_grad(h, j, t):
        return remote(
            far_s.at[h, j, t], far_r.at[h, j, t],
            far_send.at[h, j, t], far_recv.at[h, j, t], prv,
        )

    def near_grad(j, t):
        return remote(
            near_s.at[j, t], near_r.at[j, t], near_send.at[j, t], near_recv.at[j, t], prv
        )

    def x_grad(s, j, t):
        return remote(
            xs.at[s - 1, j, t], xr.at[s - 1, j, t],
            x_send.at[s - 1, j, t], x_recv.at[s - 1, j, t], beside,
        )

    def dq_copies(u):
        h, j = order[u]
        at = kv_head(u)
        own = pltpu.make_async_copy(
            dqb.at[h, j, pl.ds(c * 64, 64)], dq_out.at[:, at], dqown_sem.at[u]
        )
        away = remote(
            dqb.at[h, j, pl.ds((1 - c) * 64, 64)], dq_out.at[:, at],
            dq_send.at[u], dq_recv.at[u], twin,
        )
        return own, away

    def start(copies):
        for copy in copies:
            copy.start()

    raw_copies = [
        pltpu.make_async_copy(x, raw.at[t], raw_sem.at[t]) for t, x in enumerate((k_in, v_in))
    ]
    start(raw_copies)
    barrier = pltpu.get_barrier_semaphore()
    for peer in (twin, beside, nxt, prv):
        pl.semaphore_signal(barrier, inc=1, device_id=peer, device_id_type=MESH)
    for u in range(4):
        start(own_copies(u))
    keys = kvb.shape[4]
    for t in range(2):
        raw_copies[t].wait()
        wide[t] = raw[t].astype(jnp.float32)
        for j in range(2):
            kvb[2, p, j, t] = wide[t, pl.ds(j, keys, stride=2)].astype(jnp.bfloat16)
    pl.semaphore_wait(barrier, 4)

    for t in range(2):
        near_kv(0, t).start()
        x_kv(2, 0, t).start()
    start(qg_copies(0))
    start(qg_copies(1))

    def relay_near(j):
        for t in range(2):
            near_kv(j, t).wait_recv()
            far_kv(h1, j, t).start()
            x_kv(1, j, t).start()

    def relay_far(j):
        for t in range(2):
            x_kv(1, j, t).wait_recv()
            far_kv(1 - h1, j, t).start()

    relay_near(0)
    for t in range(2):
        near_kv(1, t).start()
        x_kv(2, 1, t).start()
    start(qg_copies(2))
    start(qg_copies(3))
    relay_far(0)

    first_token = 128 * p
    far_off = (1 - jnp.minimum(block // 2, 1)).astype(jnp.float32) * (-MASKED)
    near_off = (1 - jnp.minimum(block, 1)).astype(jnp.float32) * (-MASKED)

    def compute(u, between):
        h, j = order[u]
        for copy in own_copies(u):
            copy.wait()
        for copy in qg_copies(u):
            copy.wait_recv()
        for t in range(2):
            far_kv(h, j, t).wait_recv()
            if u in (0, 2):
                x_kv(2, j, t).wait_recv()
        unit_grads(
            [(kvb.at[s, h, j, 0], kvb.at[s, h, j, 1]) for s in range(3)],
            qb.at[h, j], gb.at[h, j], dqb.at[h, j],
            [(acc.at[s, h, j, 0], acc.at[s, h, j, 1]) for s in range(3)],
            s_ref, d_ref, first_token, far_off, near_off, between,
        )
        for t in range(2):
            far_s[h, j, t] = acc[0, h, j, t].astype(jnp.bfloat16)
            far_grad(h, j, t).start()
        start(dq_copies(u))

    def send_last(j):
        for t in range(2):
            xs[1, j, t] = acc[2, 1 - p, j, t].astype(jnp.bfloat16)
            x_grad(2, j, t).start()

    def send_middle(j):
        for t in range(2):
            far_grad(1 - h1, j, t).wait_recv()
            value = acc[1, 1 - h1, j, t] + far_r[1 - h1, j, t].astype(jnp.float32)
            xs[0, j, t] = value.astype(jnp.bfloat16)
            x_grad(1, j, t).start()

    def pass_on(j):
        for t in range(2):
            far_grad(h1, j, t).wait_recv()
            x_grad(1, j, t).wait_recv()
            value = acc[1, h1, j, t] + far_r[h1, j, t].astype(jnp.float32)
            value = value + xr[0, j, t].astype(jnp.float32)
            near_s[j, t] = value.astype(jnp.bfloat16)
            near_grad(j, t).start()

    def finish(j):
        for t in range(2):
            x_grad(2, j, t).wait_recv()
            near_grad(j, t).wait_recv()
            value = acc[2, p, j, t] + xr[1, j, t].astype(jnp.float32)
            value = value + near_r[j, t].astype(jnp.float32)
            wide[t, pl.ds(j, keys, stride=2)] = value

    def nothing():
        pass

    compute(0, functools.partial(relay_near, 1))
    compute(1, functools.partial(relay_far, 1))
    send_last(0)
    compute(2, nothing)
    compute(3, functools.partial(send_middle, 0))
    send_last(1)
    pass_on(0)
    send_middle(1)
    pass_on(1)
    finish(0)
    finish(1)
    dk_out[...] = wide[0].astype(jnp.bfloat16)
    dv_out[...] = wide[1].astype(jnp.bfloat16)

    for u in range(4):
        own, away = dq_copies(u)
        own.wait()
        away.wait_recv()
        away.wait_send()
        for copy in qg_copies(u):
            copy.wait_send()
    for j in range(2):
        for t in range(2):
            near_kv(j, t).wait_send()
            near_grad(j, t).wait_send()
            for s in (1, 2):
                x_kv(s, j, t).wait_send()
                x_grad(s, j, t).wait_send()
            for h in range(2):
                far_kv(h, j, t).wait_send()
                far_grad(h, j, t).wait_send()


def shards(sizes, queries, key_rows, value_rows, grad_out):
    tokens, heads, width = queries.shape
    keys, groups, _ = key_rows.shape
    split = (tokens, 8, heads // 8, width)
    bf16, f32 = jnp.bfloat16, jnp.float32
    any_space = pl.BlockSpec(memory_space=pl.ANY)
    vmem = pl.BlockSpec(memory_space=pltpu.VMEM)
    dma = pltpu.SemaphoreType.DMA
    unit = (2, 2, 2 * tokens, heads // 8, width)
    pieces = (2, 2, keys, width)
    eight, four = dma((2, 2, 2)), dma((2, 2))
    flat = (groups * keys, width)
    dq, dk, dv = pl.pallas_call(
        functools.partial(kernel, sizes),
        out_shape=(
            jax.ShapeDtypeStruct(split, bf16),
            jax.ShapeDtypeStruct(flat, bf16),
            jax.ShapeDtypeStruct(flat, bf16),
        ),
        in_specs=[any_space] * 4,
        out_specs=(any_space, vmem, vmem),
        scratch_shapes=[
            pltpu.VMEM((3, 2) + pieces, bf16),
            pltpu.VMEM(unit, bf16),
            pltpu.VMEM(unit, bf16),
            pltpu.VMEM(unit, bf16),
            pltpu.VMEM((3, 2) + pieces, f32),
            pltpu.VMEM((3, keys, ROWS), f32),
            pltpu.VMEM((3, keys, ROWS), f32),
            pltpu.VMEM((2,) + flat, bf16),
            pltpu.VMEM((2,) + flat, f32),
            pltpu.VMEM((2,) + pieces, bf16),
            pltpu.VMEM((2,) + pieces, bf16),
            pltpu.VMEM(pieces, bf16),
            pltpu.VMEM(pieces, bf16),
            pltpu.VMEM((2,) + pieces, bf16),
            pltpu.VMEM((2,) + pieces, bf16),
            dma((2,)), dma((4, 2)), dma((4, 2)), dma((4, 2)),
            four, four, eight, eight, eight, eight,
            dma((4,)), dma((4,)), dma((4,)),
            eight, eight, four, four, eight, eight,
        ],
        compiler_params=pltpu.CompilerParams(collective_id=0, has_side_effects=True),
        name="window_grads",
    )(
        queries.reshape(split), grad_out.reshape(split),
        key_rows.reshape(flat), value_rows.reshape(flat),
    )
    return dq.reshape(queries.shape), dk.reshape(key_rows.shape), dv.reshape(key_rows.shape)


def solution(mesh):
    rows = P(("inner", "outer", "head"), None, None)
    groups = P(("inner", "outer"), "head", None)
    return jax.shard_map(
        functools.partial(shards, (mesh.shape["inner"], mesh.shape["outer"])),
        mesh=mesh,
        in_specs=(rows, groups, groups, rows),
        out_specs=(rows, groups, groups),
        check_vma=False,
    )
```

```python
import functools

import jax
import jax.numpy as jnp
from jax import lax
from jax.experimental import pallas as pl
from jax.experimental.pallas import tpu as pltpu
from jax.sharding import PartitionSpec as P

MESH = pl.DeviceIdType.MESH
SCALE = 128**-0.5
LOG2E = 1.4426950408889634
MASKED = -1e30
ROWS = 512


PIECES = 4


def dot(a, b, a_dim, b_dim):
    return lax.dot_general(
        a, b, (((a_dim,), (b_dim,)), ((), ())), preferred_element_type=jnp.float32
    )


def rows_of(ref):
    return ref[...].reshape(-1, ref.shape[-1])


def unit_grads(kv, q_ref, g_ref, dq_ref, acc, s_ref, d_ref, first_token, far_off, near_off, between, first_done):
    offs = (far_off, near_off, None)
    tokens, heads, width = q_ref.shape
    per = ROWS // heads
    for i in range(tokens // per):
        if i:
            between()
        part = pl.ds(i * per, per)
        q = q_ref[part].reshape(ROWS, width)
        g = g_ref[part].reshape(ROWS, width)
        highest = None
        for s in range(3):
            x = dot(rows_of(kv[s][0]), q, 1, 1)
            if s == 2:
                key = lax.broadcasted_iota(jnp.int32, x.shape, 0) * heads
                row = lax.broadcasted_iota(jnp.int32, x.shape, 1)
                x = jnp.where(key - row <= heads * first_token + i * ROWS, x, MASKED)
            s_ref[s] = x
            top = jnp.max(x, axis=0, keepdims=True)
            if offs[s] is not None:
                top = top - offs[s]
            highest = top if highest is None else jnp.maximum(highest, top)
        total = jnp.zeros((1, ROWS), jnp.float32)
        delta = jnp.zeros((1, ROWS), jnp.float32)
        for s in range(3):
            base = highest if offs[s] is None else highest + offs[s]
            e = jnp.exp2((s_ref[s] - base) * (SCALE * LOG2E))
            s_ref[s] = e
            total = total + jnp.sum(e, axis=0, keepdims=True)
            dp = dot(rows_of(kv[s][1]), g, 1, 1)
            d_ref[s] = dp
            delta = delta + jnp.sum(e * dp, axis=0, keepdims=True)
        inverse = 1.0 / total
        delta = delta * inverse
        dq = None
        for s in range(3):
            probs = s_ref[s] * inverse
            low = probs.astype(jnp.bfloat16)
            ds = (probs * (d_ref[s] - delta)).astype(jnp.bfloat16)
            dv = dot(low, g, 1, 0)
            dk = dot(ds, q, 1, 0) * SCALE
            if i == 0:
                acc[s][1][...] = dv
                acc[s][0][...] = dk
            else:
                acc[s][1][...] += dv
                acc[s][0][...] += dk
            if s == 0 and i == tokens // per - 1:
                first_done()
            term = dot(ds, rows_of(kv[s][0]), 0, 0)
            dq = term if dq is None else dq + term
        dq_ref[part] = (dq * SCALE).astype(jnp.bfloat16).reshape(per, heads, width)


def kernel(
    sizes,
    q_in, g_in, k_in, v_in,
    dq_out, dk_out, dv_out,
    kvb, qb, gb, dqb, acc, s_ref, d_ref, raw, wide,
    far_s, far_r, near_s, near_r, xs, xr,
    raw_sem, own_sem, qg_send, qg_recv,
    near_kv_send, near_kv_recv, far_kv_send, far_kv_recv, x_kv_send, x_kv_recv,
    dqown_sem, dq_send, dq_recv,
    far_send, far_recv, near_send, near_recv, x_send, x_recv,
):
    n_inner, n_outer = sizes
    n_z = n_outer // 2
    blocks = n_inner * n_outer
    inner, outer, head = lax.axis_index("inner"), lax.axis_index("outer"), lax.axis_index("head")
    p, c = head // 2, head % 2
    z = outer % n_z
    block = inner * n_outer + outer
    turn_next = 1 - jnp.minimum(n_z - 1 - z, 1)
    turn_here = 1 - jnp.minimum(z, 1)
    turn_prev = 1 - jnp.minimum((z - 1) * (z - 1), 1)
    a = (p + turn_here + turn_prev) % 2
    h1 = (p + turn_here) % 2

    def place(b, pp):
        return (b // n_outer, b % n_outer, pp * 2 + c)

    nxt = place((block + 1) % blocks, (p + turn_next) % 2)
    prv = place((block + blocks - 1) % blocks, (p + turn_here) % 2)
    beside = (inner, outer, (1 - p) * 2 + c)
    twin = (inner, outer, p * 2 + 1 - c)
    order = ((a, 0), (1 - a, 0), (a, 1), (1 - a, 1))

    def kv_head(u):
        h, j = order[u]
        return 4 * h + 2 * c + j

    def remote(src, dst, send, recv, device):
        return pltpu.make_async_remote_copy(
            src_ref=src, dst_ref=dst, send_sem=send, recv_sem=recv,
            device_id=device, device_id_type=MESH,
        )

    def own_copies(u):
        h, j = order[u]
        to = pl.ds(c * 64, 64)
        return [
            pltpu.make_async_copy(q_in.at[:, kv_head(u)], qb.at[h, j, to], own_sem.at[u, 0]),
            pltpu.make_async_copy(g_in.at[:, kv_head(u)], gb.at[h, j, to], own_sem.at[u, 1]),
        ]

    def qg_copies(u):
        h, j = order[u]
        there = 4 * h + 2 * (1 - c) + j
        to = pl.ds(c * 64, 64)
        return [
            remote(q_in.at[:, there], qb.at[h, j, to], qg_send.at[u, 0], qg_recv.at[u, 0], twin),
            remote(g_in.at[:, there], gb.at[h, j, to], qg_send.at[u, 1], qg_recv.at[u, 1], twin),
        ]

    def near_kv(j, i):
        return remote(
            kvb.at[2, p, j, i], kvb.at[1, p, j, i],
            near_kv_send.at[j, i], near_kv_recv.at[j, i], nxt,
        )

    def far_kv(h, j, i):
        return remote(
            kvb.at[1, h, j, i], kvb.at[0, h, j, i],
            far_kv_send.at[h, j, i], far_kv_recv.at[h, j, i], nxt,
        )

    def x_kv(s, j, i):
        piece = kvb.at[s, p if s == 2 else h1, j, i]
        return remote(piece, piece, x_kv_send.at[s - 1, j, i], x_kv_recv.at[s - 1, j, i], beside)

    def far_grad(h, j, i):
        return remote(
            far_s.at[h, j, i], far_r.at[h, j, i],
            far_send.at[h, j, i], far_recv.at[h, j, i], prv,
        )

    def near_grad(j, i):
        return remote(
            near_s.at[j, i], near_r.at[j, i], near_send.at[j, i], near_recv.at[j, i], prv
        )

    def x_grad(s, j, i):
        return remote(
            xs.at[s - 1, j, i], xr.at[s - 1, j, i],
            x_send.at[s - 1, j, i], x_recv.at[s - 1, j, i], beside,
        )

    def dq_copies(u):
        h, j = order[u]
        at = kv_head(u)
        own = pltpu.make_async_copy(
            dqb.at[h, j, pl.ds(c * 64, 64)], dq_out.at[:, at], dqown_sem.at[u]
        )
        away = remote(
            dqb.at[h, j, pl.ds((1 - c) * 64, 64)], dq_out.at[:, at],
            dq_send.at[u], dq_recv.at[u], twin,
        )
        return own, away

    def start(copies):
        for copy in copies:
            copy.start()

    raw_copies = [
        pltpu.make_async_copy(x, raw.at[t], raw_sem.at[t]) for t, x in enumerate((k_in, v_in))
    ]
    start(raw_copies)
    barrier = pltpu.get_barrier_semaphore()
    for peer in (twin, beside, nxt, prv):
        pl.semaphore_signal(barrier, inc=1, device_id=peer, device_id_type=MESH)
    for u in range(4):
        start(own_copies(u))
    size = kvb.shape[4]

    def at(i):
        return i // 2, pl.ds(i % 2 * size, size)

    def alternate(i, j):
        return i // 2, pl.ds(i % 2 * 2 * size + j, size, stride=2)

    for t in range(2):
        raw_copies[t].wait()
        wide[t] = raw[t].astype(jnp.float32)
    for j in range(2):
        for i in range(PIECES):
            kvb[2, p, j, i] = wide[alternate(i, j)].astype(jnp.bfloat16)
    pl.semaphore_wait(barrier, 4)

    for i in range(PIECES):
        near_kv(0, i).start()
        x_kv(2, 0, i).start()
    start(qg_copies(0))
    start(qg_copies(1))

    def relay_near(j):
        for i in range(PIECES):
            near_kv(j, i).wait_recv()
            far_kv(h1, j, i).start()
            x_kv(1, j, i).start()

    def relay_far(j):
        for i in range(PIECES):
            x_kv(1, j, i).wait_recv()
            far_kv(1 - h1, j, i).start()

    relay_near(0)
    for i in range(PIECES):
        near_kv(1, i).start()
        x_kv(2, 1, i).start()
    start(qg_copies(2))
    start(qg_copies(3))
    relay_far(0)

    first_token = 128 * p
    far_off = (1 - jnp.minimum(block // 2, 1)).astype(jnp.float32) * (-MASKED)
    near_off = (1 - jnp.minimum(block, 1)).astype(jnp.float32) * (-MASKED)

    def send_first(h, j):
        for i in range(PIECES):
            far_s[h, j, i] = acc[(0, h, j) + at(i)].astype(jnp.bfloat16)
            far_grad(h, j, i).start()

    def compute(u, between):
        h, j = order[u]
        for copy in own_copies(u):
            copy.wait()
        for copy in qg_copies(u):
            copy.wait_recv()
        for i in range(PIECES):
            far_kv(h, j, i).wait_recv()
            if u in (0, 2):
                x_kv(2, j, i).wait_recv()
        unit_grads(
            [(kvb.at[s, h, j, pl.ds(0, 2)], kvb.at[s, h, j, pl.ds(2, 2)]) for s in range(3)],
            qb.at[h, j], gb.at[h, j], dqb.at[h, j],
            [(acc.at[s, h, j, 0], acc.at[s, h, j, 1]) for s in range(3)],
            s_ref, d_ref, first_token, far_off, near_off, between,
            functools.partial(send_first, h, j),
        )
        start(dq_copies(u))

    def send_last(j):
        for i in range(PIECES):
            xs[1, j, i] = acc[(2, 1 - p, j) + at(i)].astype(jnp.bfloat16)
            x_grad(2, j, i).start()

    def send_middle(j):
        for i in range(PIECES):
            far_grad(1 - h1, j, i).wait_recv()
            value = acc[(1, 1 - h1, j) + at(i)] + far_r[1 - h1, j, i].astype(jnp.float32)
            xs[0, j, i] = value.astype(jnp.bfloat16)
            x_grad(1, j, i).start()

    def pass_on(j):
        for i in range(PIECES):
            far_grad(h1, j, i).wait_recv()
            x_grad(1, j, i).wait_recv()
            value = acc[(1, h1, j) + at(i)] + far_r[h1, j, i].astype(jnp.float32)
            value = value + xr[0, j, i].astype(jnp.float32)
            near_s[j, i] = value.astype(jnp.bfloat16)
            near_grad(j, i).start()

    def finish(j):
        for i in range(PIECES):
            x_grad(2, j, i).wait_recv()
            near_grad(j, i).wait_recv()
            value = acc[(2, p, j) + at(i)] + xr[1, j, i].astype(jnp.float32)
            value = value + near_r[j, i].astype(jnp.float32)
            wide[alternate(i, j)] = value

    def nothing():
        pass

    compute(0, functools.partial(relay_near, 1))
    compute(1, functools.partial(relay_far, 1))
    send_last(0)
    compute(2, nothing)
    compute(3, functools.partial(send_middle, 0))
    send_last(1)
    pass_on(0)
    send_middle(1)
    pass_on(1)
    finish(0)
    finish(1)
    result_copies = []
    for t, out in enumerate((dk_out, dv_out)):
        raw[t] = wide[t].astype(jnp.bfloat16)
        result_copies.append(pltpu.make_async_copy(raw.at[t], out, raw_sem.at[t]))
    start(result_copies)

    for copy in result_copies:
        copy.wait()
    for u in range(4):
        own, away = dq_copies(u)
        own.wait()
        away.wait_recv()
        away.wait_send()
        for copy in qg_copies(u):
            copy.wait_send()
    for j in range(2):
        for i in range(PIECES):
            near_kv(j, i).wait_send()
            near_grad(j, i).wait_send()
            for s in (1, 2):
                x_kv(s, j, i).wait_send()
                x_grad(s, j, i).wait_send()
            for h in range(2):
                far_kv(h, j, i).wait_send()
                far_grad(h, j, i).wait_send()


def shards(sizes, queries, key_rows, value_rows, grad_out):
    tokens, heads, width = queries.shape
    keys, groups, _ = key_rows.shape
    split = (tokens, 8, heads // 8, width)
    bf16, f32 = jnp.bfloat16, jnp.float32
    any_space = pl.BlockSpec(memory_space=pl.ANY)
    hbm = pl.BlockSpec(memory_space=pltpu.HBM)
    dma = pltpu.SemaphoreType.DMA
    unit = (2, 2, 2 * tokens, heads // 8, width)
    pieces = (2, PIECES, keys // 2, width)
    many, some = dma((2, 2, PIECES)), dma((2, PIECES))
    flat = (groups * keys, width)
    dq, dk, dv = pl.pallas_call(
        functools.partial(kernel, sizes),
        out_shape=(
            pltpu.VMEM(split, bf16),
            pltpu.VMEM(flat, bf16),
            pltpu.VMEM(flat, bf16),
        ),
        in_specs=[hbm] * 4,
        out_specs=(any_space, any_space, any_space),
        scratch_shapes=[
            pltpu.VMEM((3, 2) + pieces, bf16),
            pltpu.VMEM(unit, bf16),
            pltpu.VMEM(unit, bf16),
            pltpu.VMEM(unit, bf16),
            pltpu.VMEM((3, 2, 2, 2, keys, width), f32),
            pltpu.VMEM((3, keys, ROWS), f32),
            pltpu.VMEM((3, keys, ROWS), f32),
            pltpu.VMEM((2,) + flat, bf16),
            pltpu.VMEM((2,) + flat, f32),
            pltpu.VMEM((2,) + pieces, bf16),
            pltpu.VMEM((2,) + pieces, bf16),
            pltpu.VMEM(pieces, bf16),
            pltpu.VMEM(pieces, bf16),
            pltpu.VMEM((2,) + pieces, bf16),
            pltpu.VMEM((2,) + pieces, bf16),
            dma((2,)), dma((4, 2)), dma((4, 2)), dma((4, 2)),
            some, some, many, many, many, many,
            dma((4,)), dma((4,)), dma((4,)),
            many, many, some, some, many, many,
        ],
        compiler_params=pltpu.CompilerParams(
            collective_id=0, has_side_effects=True, vmem_limit_bytes=60 * 2**20
        ),
        name="window_grads",
    )(
        queries.reshape(split), grad_out.reshape(split),
        key_rows.reshape(flat), value_rows.reshape(flat),
    )
    return dq.reshape(queries.shape), dk.reshape(key_rows.shape), dv.reshape(key_rows.shape)


def solution(mesh):
    rows = P(("inner", "outer", "head"), None, None)
    groups = P(("inner", "outer"), "head", None)
    return jax.shard_map(
        functools.partial(shards, (mesh.shape["inner"], mesh.shape["outer"])),
        mesh=mesh,
        in_specs=(rows, groups, groups, rows),
        out_specs=(rows, groups, groups),
        check_vma=False,
    )
```

```python
import functools

import jax
import jax.numpy as jnp
from jax import lax
from jax.experimental import pallas as pl
from jax.experimental.pallas import tpu as pltpu
from jax.sharding import PartitionSpec as P

MESH = pl.DeviceIdType.MESH
SCALE = 128**-0.5
LOG2E = 1.4426950408889634
MASKED = -1e30
ROWS = 512


PIECES = 4


def dot(a, b, a_dim, b_dim):
    return lax.dot_general(
        a, b, (((a_dim,), (b_dim,)), ((), ())), preferred_element_type=jnp.float32
    )


def rows_of(ref):
    return ref[...].reshape(-1, ref.shape[-1])


def unit_grads(kv, q_ref, g_ref, dq_ref, acc, s_ref, d_ref, first_token, far_off, near_off, between, first_done):
    offs = (far_off, near_off, None)
    tokens, heads, width = q_ref.shape
    per = ROWS // heads
    for i in range(tokens // per):
        if i:
            between()
        part = pl.ds(i * per, per)
        q = q_ref[part].reshape(ROWS, width)
        g = g_ref[part].reshape(ROWS, width)
        highest = None
        for s in range(3):
            x = dot(rows_of(kv[s][0]), q, 1, 1)
            if s == 2:
                key = lax.broadcasted_iota(jnp.int32, x.shape, 0) * heads
                row = lax.broadcasted_iota(jnp.int32, x.shape, 1)
                x = jnp.where(key - row <= heads * first_token + i * ROWS, x, MASKED)
            s_ref[s] = x
            top = jnp.max(x, axis=0, keepdims=True)
            if offs[s] is not None:
                top = top - offs[s]
            highest = top if highest is None else jnp.maximum(highest, top)
        total = jnp.zeros((1, ROWS), jnp.float32)
        delta = jnp.zeros((1, ROWS), jnp.float32)
        for s in range(3):
            base = highest if offs[s] is None else highest + offs[s]
            e = jnp.exp2((s_ref[s] - base) * (SCALE * LOG2E))
            s_ref[s] = e
            total = total + jnp.sum(e, axis=0, keepdims=True)
            dp = dot(rows_of(kv[s][1]), g, 1, 1)
            d_ref[s] = dp
            delta = delta + jnp.sum(e * dp, axis=0, keepdims=True)
        inverse = 1.0 / total
        delta = delta * inverse
        dq = None
        for s in range(3):
            probs = s_ref[s] * inverse
            low = probs.astype(jnp.bfloat16)
            ds = (probs * (d_ref[s] - delta)).astype(jnp.bfloat16)
            dv = dot(low, g, 1, 0)
            dk = dot(ds, q, 1, 0) * SCALE
            if i == 0:
                acc[s][1][...] = dv
                acc[s][0][...] = dk
            else:
                acc[s][1][...] += dv
                acc[s][0][...] += dk
            if s == 0 and i == tokens // per - 1:
                first_done()
            term = dot(ds, rows_of(kv[s][0]), 0, 0)
            dq = term if dq is None else dq + term
        dq_ref[part] = (dq * SCALE).astype(jnp.bfloat16).reshape(per, heads, width)


def kernel(
    sizes,
    q_in, g_in, k_in, v_in,
    dq_out, dk_out, dv_out,
    kvb, qb, gb, dqb, acc, s_ref, d_ref, raw, wide,
    far_s, far_r, near_s, near_r, xs, xr,
    raw_sem, own_sem, qg_send, qg_recv,
    near_kv_send, near_kv_recv, far_kv_send, far_kv_recv, x_kv_send, x_kv_recv,
    dqown_sem, dq_send, dq_recv,
    far_send, far_recv, near_send, near_recv, x_send, x_recv,
):
    n_inner, n_outer = sizes
    n_z = n_outer // 2
    blocks = n_inner * n_outer
    inner, outer, head = lax.axis_index("inner"), lax.axis_index("outer"), lax.axis_index("head")
    p, c = head // 2, head % 2
    z = outer % n_z
    block = inner * n_outer + outer
    turn_next = 1 - jnp.minimum(n_z - 1 - z, 1)
    turn_here = 1 - jnp.minimum(z, 1)
    turn_prev = 1 - jnp.minimum((z - 1) * (z - 1), 1)
    a = (p + turn_here + turn_prev) % 2
    h1 = (p + turn_here) % 2

    def place(b, pp):
        return (b // n_outer, b % n_outer, pp * 2 + c)

    nxt = place((block + 1) % blocks, (p + turn_next) % 2)
    prv = place((block + blocks - 1) % blocks, (p + turn_here) % 2)
    beside = (inner, outer, (1 - p) * 2 + c)
    twin = (inner, outer, p * 2 + 1 - c)
    order = ((a, 0), (1 - a, 0), (a, 1), (1 - a, 1))

    def kv_head(u):
        h, j = order[u]
        return 4 * h + 2 * c + j

    def remote(src, dst, send, recv, device):
        return pltpu.make_async_remote_copy(
            src_ref=src, dst_ref=dst, send_sem=send, recv_sem=recv,
            device_id=device, device_id_type=MESH,
        )

    def own_copies(u):
        h, j = order[u]
        to = pl.ds(c * 64, 64)
        return [
            pltpu.make_async_copy(q_in.at[:, kv_head(u)], qb.at[h, j, to], own_sem.at[u, 0]),
            pltpu.make_async_copy(g_in.at[:, kv_head(u)], gb.at[h, j, to], own_sem.at[u, 1]),
        ]

    def qg_copies(u):
        h, j = order[u]
        there = 4 * h + 2 * (1 - c) + j
        to = pl.ds(c * 64, 64)
        return [
            remote(q_in.at[:, there], qb.at[h, j, to], qg_send.at[u, 0], qg_recv.at[u, 0], twin),
            remote(g_in.at[:, there], gb.at[h, j, to], qg_send.at[u, 1], qg_recv.at[u, 1], twin),
        ]

    def near_kv(j, i):
        return remote(
            kvb.at[2, p, j, i], kvb.at[1, p, j, i],
            near_kv_send.at[j, i], near_kv_recv.at[j, i], nxt,
        )

    def far_kv(h, j, i):
        return remote(
            kvb.at[1, h, j, i], kvb.at[0, h, j, i],
            far_kv_send.at[h, j, i], far_kv_recv.at[h, j, i], nxt,
        )

    def x_kv(s, j, i):
        piece = kvb.at[s, (a, h1, p)[s], j, i]
        return remote(piece, piece, x_kv_send.at[s, j, i], x_kv_recv.at[s, j, i], beside)

    def far_grad(h, j, i):
        return remote(
            far_s.at[h, j, i], far_r.at[h, j, i],
            far_send.at[h, j, i], far_recv.at[h, j, i], prv,
        )

    def near_grad(j, i):
        return remote(
            near_s.at[j, i], near_r.at[j, i], near_send.at[j, i], near_recv.at[j, i], prv
        )

    def x_grad(s, j, i):
        return remote(
            xs.at[s - 1, j, i], xr.at[s - 1, j, i],
            x_send.at[s - 1, j, i], x_recv.at[s - 1, j, i], beside,
        )

    def dq_copies(u):
        h, j = order[u]
        at = kv_head(u)
        own = pltpu.make_async_copy(
            dqb.at[h, j, pl.ds(c * 64, 64)], dq_out.at[:, at], dqown_sem.at[u]
        )
        away = remote(
            dqb.at[h, j, pl.ds((1 - c) * 64, 64)], dq_out.at[:, at],
            dq_send.at[u], dq_recv.at[u], twin,
        )
        return own, away

    def start(copies):
        for copy in copies:
            copy.start()

    raw_copies = [
        pltpu.make_async_copy(x, raw.at[t], raw_sem.at[t]) for t, x in enumerate((k_in, v_in))
    ]
    start(raw_copies)
    barrier = pltpu.get_barrier_semaphore()
    for peer in (twin, beside, nxt, prv):
        pl.semaphore_signal(barrier, inc=1, device_id=peer, device_id_type=MESH)
    for u in range(4):
        start(own_copies(u))
    size = kvb.shape[4]

    def at(i):
        return i // 2, pl.ds(i % 2 * size, size)

    def alternate(i, j):
        return i // 2, pl.ds(i % 2 * 2 * size + j, size, stride=2)

    for t in range(2):
        raw_copies[t].wait()
        wide[t] = raw[t].astype(jnp.float32)
    for j in range(2):
        for i in range(PIECES):
            kvb[2, p, j, i] = wide[alternate(i, j)].astype(jnp.bfloat16)
    pl.semaphore_wait(barrier, 4)

    for i in range(PIECES):
        near_kv(0, i).start()
        x_kv(2, 0, i).start()
    start(qg_copies(0))
    start(qg_copies(1))

    def relay_near(j):
        for i in range(PIECES):
            near_kv(j, i).wait_recv()
            far_kv(h1, j, i).start()
            x_kv(1, j, i).start()

    def second_arrivals():
        relay_near(1)
        for i in range(PIECES):
            x_kv(2, 1, i).start()

    def relay_far():
        for i in range(PIECES):
            x_kv(1, 1, i).wait_recv()
            far_kv(1 - h1, 1, i).start()

    relay_near(0)
    for i in range(PIECES):
        near_kv(1, i).start()
    start(qg_copies(2))
    start(qg_copies(3))
    for i in range(PIECES):
        far_kv(a, 0, i).wait_recv()
        x_kv(0, 0, i).start()
    for i in range(PIECES):
        x_kv(1, 0, i).wait_recv()

    first_token = 128 * p
    far_off = (1 - jnp.minimum(block // 2, 1)).astype(jnp.float32) * (-MASKED)
    near_off = (1 - jnp.minimum(block, 1)).astype(jnp.float32) * (-MASKED)

    def send_first(h, j):
        for i in range(PIECES):
            far_s[h, j, i] = acc[(0, h, j) + at(i)].astype(jnp.bfloat16)
            far_grad(h, j, i).start()

    def compute(u, between):
        h, j = order[u]
        for copy in own_copies(u):
            copy.wait()
        for copy in qg_copies(u):
            copy.wait_recv()
        for i in range(PIECES):
            if u == 1:
                x_kv(0, 0, i).wait_recv()
            elif u > 1:
                far_kv(h, j, i).wait_recv()
            if j != order[u - 1][1]:
                x_kv(2, j, i).wait_recv()
        unit_grads(
            [(kvb.at[s, h, j, pl.ds(0, 2)], kvb.at[s, h, j, pl.ds(2, 2)]) for s in range(3)],
            qb.at[h, j], gb.at[h, j], dqb.at[h, j],
            [(acc.at[s, h, j, 0], acc.at[s, h, j, 1]) for s in range(3)],
            s_ref, d_ref, first_token, far_off, near_off, between,
            functools.partial(send_first, h, j),
        )
        start(dq_copies(u))

    def send_last(j):
        for i in range(PIECES):
            xs[1, j, i] = acc[(2, 1 - p, j) + at(i)].astype(jnp.bfloat16)
            x_grad(2, j, i).start()

    def send_middle(j):
        for i in range(PIECES):
            far_grad(1 - h1, j, i).wait_recv()
            value = acc[(1, 1 - h1, j) + at(i)] + far_r[1 - h1, j, i].astype(jnp.float32)
            xs[0, j, i] = value.astype(jnp.bfloat16)
            x_grad(1, j, i).start()

    def pass_on(j):
        for i in range(PIECES):
            far_grad(h1, j, i).wait_recv()
            x_grad(1, j, i).wait_recv()
            value = acc[(1, h1, j) + at(i)] + far_r[h1, j, i].astype(jnp.float32)
            value = value + xr[0, j, i].astype(jnp.float32)
            near_s[j, i] = value.astype(jnp.bfloat16)
            near_grad(j, i).start()

    def finish(j):
        for i in range(PIECES):
            x_grad(2, j, i).wait_recv()
            near_grad(j, i).wait_recv()
            value = acc[(2, p, j) + at(i)] + xr[1, j, i].astype(jnp.float32)
            value = value + near_r[j, i].astype(jnp.float32)
            wide[alternate(i, j)] = value

    def nothing():
        pass

    compute(0, second_arrivals)
    compute(1, relay_far)
    send_last(0)
    compute(2, nothing)
    compute(3, functools.partial(send_middle, 0))
    send_last(1)
    pass_on(0)
    send_middle(1)
    pass_on(1)
    finish(0)
    finish(1)
    result_copies = []
    for t, out in enumerate((dk_out, dv_out)):
        raw[t] = wide[t].astype(jnp.bfloat16)
        result_copies.append(pltpu.make_async_copy(raw.at[t], out, raw_sem.at[t]))
    start(result_copies)

    for copy in result_copies:
        copy.wait()
    for u in range(4):
        own, away = dq_copies(u)
        own.wait()
        away.wait_recv()
        away.wait_send()
        for copy in qg_copies(u):
            copy.wait_send()
    for j in range(2):
        for i in range(PIECES):
            near_kv(j, i).wait_send()
            near_grad(j, i).wait_send()
            for s in (1, 2):
                x_kv(s, j, i).wait_send()
                x_grad(s, j, i).wait_send()
            far_kv(h1, j, i).wait_send()
            (x_kv(0, j, i) if j == 0 else far_kv(1 - h1, j, i)).wait_send()
            for h in range(2):
                far_grad(h, j, i).wait_send()


def write_out(*refs):
    ins, outs, sems = refs[:3], refs[3:6], refs[6]
    copies = [pltpu.make_async_copy(a, b, sems.at[n]) for n, (a, b) in enumerate(zip(ins, outs))]
    for copy in copies:
        copy.start()
    for copy in copies:
        copy.wait()


def shards(sizes, queries, key_rows, value_rows, grad_out):
    tokens, heads, width = queries.shape
    keys, groups, _ = key_rows.shape
    split = (tokens, 8, heads // 8, width)
    bf16, f32 = jnp.bfloat16, jnp.float32
    any_space = pl.BlockSpec(memory_space=pl.ANY)
    hbm = pl.BlockSpec(memory_space=pltpu.HBM)
    dma = pltpu.SemaphoreType.DMA
    unit = (2, 2, 2 * tokens, heads // 8, width)
    pieces = (2, PIECES, keys // 2, width)
    many, some = dma((2, 2, PIECES)), dma((2, PIECES))
    flat = (groups * keys, width)
    dq, dk, dv = pl.pallas_call(
        functools.partial(kernel, sizes),
        out_shape=(
            pltpu.VMEM(split, bf16),
            pltpu.VMEM(flat, bf16),
            pltpu.VMEM(flat, bf16),
        ),
        in_specs=[hbm] * 4,
        out_specs=(any_space, any_space, any_space),
        scratch_shapes=[
            pltpu.VMEM((3, 2) + pieces, bf16),
            pltpu.VMEM(unit, bf16),
            pltpu.VMEM(unit, bf16),
            pltpu.VMEM(unit, bf16),
            pltpu.VMEM((3, 2, 2, 2, keys, width), f32),
            pltpu.VMEM((3, keys, ROWS), f32),
            pltpu.VMEM((3, keys, ROWS), f32),
            pltpu.VMEM((2,) + flat, bf16),
            pltpu.VMEM((2,) + flat, f32),
            pltpu.VMEM((2,) + pieces, bf16),
            pltpu.VMEM((2,) + pieces, bf16),
            pltpu.VMEM(pieces, bf16),
            pltpu.VMEM(pieces, bf16),
            pltpu.VMEM((2,) + pieces, bf16),
            pltpu.VMEM((2,) + pieces, bf16),
            dma((2,)), dma((4, 2)), dma((4, 2)), dma((4, 2)),
            some, some, many, many, dma((3, 2, PIECES)), dma((3, 2, PIECES)),
            dma((4,)), dma((4,)), dma((4,)),
            many, many, some, some, many, many,
        ],
        compiler_params=pltpu.CompilerParams(
            collective_id=0, has_side_effects=True, vmem_limit_bytes=60 * 2**20
        ),
        name="window_grads",
    )(
        queries.reshape(split), grad_out.reshape(split),
        key_rows.reshape(flat), value_rows.reshape(flat),
    )
    dq, dk, dv = pl.pallas_call(
        write_out,
        out_shape=(
            pltpu.HBM(split, bf16), pltpu.HBM(flat, bf16), pltpu.HBM(flat, bf16),
        ),
        in_specs=[any_space] * 3,
        out_specs=(any_space,) * 3,
        scratch_shapes=[dma((3,))],
        compiler_params=pltpu.CompilerParams(vmem_limit_bytes=2**20),
        name="write_out",
    )(dq, dk, dv)
    return dq.reshape(queries.shape), dk.reshape(key_rows.shape), dv.reshape(key_rows.shape)


def solution(mesh):
    rows = P(("inner", "outer", "head"), None, None)
    groups = P(("inner", "outer"), "head", None)
    return jax.shard_map(
        functools.partial(shards, (mesh.shape["inner"], mesh.shape["outer"])),
        mesh=mesh,
        in_specs=(rows, groups, groups, rows),
        out_specs=(rows, groups, groups),
        check_vma=False,
    )
```
